32 devices in a mesh: dp: 2 (over core), seq: 4 (over z), tensor: 4 (over y, x).
Axes of the slice: x: 2, y: 2, z: 4, core: 2. Of those that a mesh axis runs over, the one named last changes fastest.
Arguments:
- x_in: bfloat16 [2, 2, 1024, 2560], P(None, 'dp', 'seq'), may hold values from -6 to 6
- cotangent: bfloat16 [2, 2, 1024, 2560], P(None, 'dp', 'seq'), may hold values from -6 to 6
- gain_mix: float32 [2560], replicated, may hold values from 0.5 to 1.5
- w_in: bfloat16 [2, 2560, 2560], P(None, ('dp', 'seq'), 'tensor'), may hold values from -0.125 to 0.125
- b_in: float32 [2, 2560], P(None, 'tensor'), may hold values from -3 to 3
- conv_w: float32 [4, 2560], P(None, 'tensor'), may hold values from -3 to 3
- conv_b: float32 [2560], P('tensor'), may hold values from -2 to 2
- w_gates: bfloat16 [2, 256, 2560], P(None, ('dp', 'seq'), 'tensor'), may hold values from -0.375 to 0.375
- b_gates: float32 [2, 2560], P(None, 'tensor'), may hold values from -3 to 3
- decay_param: float32 [2560], P('tensor'), may hold values from 3 to 14
- w_out: bfloat16 [2560, 2560], P('tensor', ('dp', 'seq')), may hold values from -0.3125 to 0.3125
- b_out: float32 [2560], replicated, may hold values from -3 to 3
- gain_mlp: float32 [2560], replicated, may hold values from 0.5 to 1.5
- w_up: bfloat16 [2, 2560, 7680], P(None, ('dp', 'seq'), 'tensor'), may hold values from -0.125 to 0.125
- b_up: float32 [2, 7680], P(None, 'tensor'), may hold values from -3 to 3
- w_down: bfloat16 [7680, 2560], P('tensor', ('dp', 'seq')), may hold values from -0.09375 to 0.09375
- b_down: float32 [2560], replicated, may hold values from -3 to 3
Outputs:
- block_out: bfloat16 [2, 2, 1024, 2560], P(None, 'dp', 'seq')
- grad_input: bfloat16 [2, 2, 1024, 2560], P(None, 'dp', 'seq')
- grad_gain_mix: float32 [2560], replicated
- grad_w_in: float32 [2, 2560, 2560], P(None, ('dp', 'seq'), 'tensor')
- grad_b_in: float32 [2, 2560], P(None, 'tensor')
- grad_conv_w: float32 [4, 2560], P(None, 'tensor')
- grad_conv_b: float32 [2560], P('tensor')
- grad_w_gates: float32 [2, 256, 2560], P(None, ('dp', 'seq'), 'tensor')
- grad_b_gates: float32 [2, 2560], P(None, 'tensor')
- grad_decay_param: float32 [2560], P('tensor')
- grad_w_out: float32 [2560, 2560], P('tensor', ('dp', 'seq'))
- grad_b_out: float32 [2560], replicated
- grad_gain_mlp: float32 [2560], replicated
- grad_w_up: float32 [2, 2560, 7680], P(None, ('dp', 'seq'), 'tensor')
- grad_b_up: float32 [2, 7680], P(None, 'tensor')
- grad_w_down: float32 [7680, 2560], P('tensor', ('dp', 'seq'))
- grad_b_down: float32 [2560], replicated
The draws below stay inside these ranges and needn't reach their ends.
All inputs are finite; a program needn't handle non-finite values.
Results may differ from the reference program's by a relative error of at most 0.015.
Values may be sent and summed in bfloat16 or wider, within the bound.
No kernel may reach another device: no remote copies, remote signals or barrier semaphores. Data moves between devices by JAX's collectives and lax.ppermute only.
A program may use at most 320 MiB of HBM per device.

```python
import jax
import jax.numpy as jnp
from jax import lax

D = 2560
WIDTH = 2560
BW = 256
FF = 7680
CONV = 4
MICRO = 2
LENGTH = 1024
SEQS = 2


def draw_decay_param(key, part):
    rate_high = 0.02
    rate_low = 0.02 / LENGTH
    fraction = jax.random.uniform(key, (WIDTH,), jnp.float32)
    rate_value = jnp.exp(jnp.log(rate_low) + fraction * (jnp.log(rate_high) - jnp.log(rate_low)))
    return -jnp.log(jnp.expm1(rate_value))


def level_of(key, dims, pieces, low, top_value):
    gain, own = 1.0, jax.random.fold_in(key, 6)
    for position, shards_of in pieces:
        steps = jnp.exp(jax.random.uniform(jax.random.fold_in(own, position), (shards_of,), jnp.float32, low / len(pieces), top_value / len(pieces)))
        gain = gain * jnp.repeat(steps, dims[position] // shards_of).reshape([-1 if axis == position else 1 for axis in range(len(dims))])
    return gain


def bell_draw(own_key, extent, spread, reach, split=(), held_as=jnp.bfloat16):
    array = spread * jax.random.normal(own_key, extent, jnp.float32)
    if split:
        array = array * level_of(own_key, extent, split, -0.22, 0.18)
    return jnp.clip(array, -reach, reach).astype(held_as)


def setup_inputs(seed: int = 0) -> dict:
    key_of = jax.random.split(jax.random.key(seed), 18)
    return {
        "x_in": bell_draw(key_of[0], (MICRO, SEQS, LENGTH, D), 1.0, 6.0, ((1, 2), (2, 4))),
        "cotangent": bell_draw(key_of[1], (MICRO, SEQS, LENGTH, D), 1.0, 6.0, ((1, 2), (2, 4))),
        "gain_mix": jnp.clip(1.0 + 0.1 * jax.random.normal(key_of[2], (D,), jnp.float32), 0.5, 1.5),
        "w_in": bell_draw(key_of[3], (2, D, WIDTH), D ** -0.5, 0.125, ((1, 8), (2, 4))),
        "b_in": bell_draw(key_of[4], (2, WIDTH), 0.5, 3.0, ((1, 4),), jnp.float32),
        "conv_w": bell_draw(key_of[5], (CONV, WIDTH), 0.5, 3.0, ((1, 4),), jnp.float32),
        "conv_b": bell_draw(key_of[6], (WIDTH,), 0.3, 2.0, ((0, 4),), jnp.float32),
        "w_gates": bell_draw(key_of[7], (2, BW, WIDTH), BW ** -0.5, 0.375, ((1, 8), (2, 4))),
        "b_gates": bell_draw(key_of[8], (2, WIDTH), 0.5, 3.0, ((1, 4),), jnp.float32),
        "decay_param": draw_decay_param(jax.random.fold_in(key_of[17], 71), 0),
        "w_out": bell_draw(key_of[10], (WIDTH, D), (WIDTH // 8) ** -0.5, 0.3125, ((0, 4), (1, 8))),
        "b_out": bell_draw(key_of[11], (D,), 0.5, 3.0, (), jnp.float32),
        "gain_mlp": jnp.clip(1.0 + 0.1 * jax.random.normal(key_of[12], (D,), jnp.float32), 0.5, 1.5),
        "w_up": bell_draw(key_of[13], (2, D, FF), D ** -0.5, 0.125, ((1, 8), (2, 4))),
        "b_up": bell_draw(key_of[14], (2, FF), 0.5, 3.0, ((1, 4),), jnp.float32),
        "w_down": bell_draw(key_of[15], (FF, D), (FF // 2) ** -0.5, 0.09375, ((0, 4), (1, 8))),
        "b_down": bell_draw(key_of[16], (D,), 0.5, 3.0, (), jnp.float32),
    }


EPSILON = 1e-06
DECAY_SCALE = 8.0

@jax.custom_vjp
def low(v):
    return lax.optimization_barrier(v.astype(jnp.bfloat16)).astype(jnp.float32)

@jax.custom_vjp
def low_back(v):
    return v

def low_keep(v):
    return (low(v), None)

def low_pass(kept, grad):
    return (grad,)

def back_keep(v):
    return (v, None)

def back_low(kept, grad):
    return (low(grad),)
low.defvjp(low_keep, low_pass)
low_back.defvjp(back_keep, back_low)

def rms_scale(values, gain_vec):
    inverse = lax.rsqrt(lax.optimization_barrier(jnp.mean(values * values, axis=-1, keepdims=True)) + EPSILON)
    return values * inverse * gain_vec

def gelu_gate(gate_pre, up_pre):
    return jax.nn.gelu(gate_pre) * up_pre

def recurrence_terms(gate_rate, gate_input, inputs, decay_param, is_first):
    rate_gate = jax.nn.sigmoid(gate_rate)
    inward = jax.nn.sigmoid(gate_input)
    log_decay = -DECAY_SCALE * jax.nn.softplus(-decay_param) * rate_gate
    decays = jnp.exp(log_decay)
    factor = jnp.where(is_first, 1.0, jnp.sqrt(-jnp.expm1(2.0 * log_decay)))
    return (decays, factor * inward * inputs)

def advance(carry_state, item_pair):
    new_state = item_pair[0] * carry_state + item_pair[1]
    return (new_state, new_state)

def forward(x_seq, gain_mix, w_in, b_in, conv_w, conv_b, w_gates, b_gates, decay_param, w_out, b_out, gain_mlp, w_up, b_up, w_down, b_down):
    highest = lax.Precision.HIGHEST
    seq_len = x_seq.shape[0]
    normed = low(rms_scale(x_seq, gain_mix))
    projected = jnp.einsum('td,gdc->gtc', normed, w_in, precision=highest) + b_in[:, None, :]
    y_pre = low_back(projected[0])
    x_low = low(low_back(projected[1]))
    padded = jnp.pad(x_low, ((CONV - 1, 0), (0, 0)))
    conv_out = conv_b + conv_w[0] * padded[0:seq_len]
    for offset in range(1, CONV):
        conv_out = conv_out + conv_w[offset] * padded[offset:offset + seq_len]
    conv_out = low(conv_out)
    blocks_all = WIDTH // BW
    gate_values = jnp.einsum('tbj,gjbk->gtbk', conv_out.reshape(seq_len, blocks_all, BW), w_gates.reshape(2, BW, blocks_all, BW), precision=highest)
    gate_values = low_back(gate_values.reshape(2, seq_len, WIDTH) + b_gates[:, None, :])
    is_first = lax.broadcasted_iota(jnp.int32, (seq_len, 1), 0) == 0
    decays, drives = recurrence_terms(gate_values[0], gate_values[1], conv_out, decay_param, is_first)
    _, states = lax.scan(advance, jnp.zeros((WIDTH,), jnp.float32), (decays, drives))
    mixed_out = low(states * jax.nn.gelu(y_pre))
    residual = x_seq + low_back(jnp.dot(mixed_out, w_out, precision=highest) + b_out)
    normed_two = low(rms_scale(residual, gain_mlp))
    upper = jnp.einsum('td,gdf->gtf', normed_two, w_up, precision=highest) + b_up[:, None, :]
    gate_pre = low_back(upper[0])
    up_pre = low_back(upper[1])
    hidden = low(gelu_gate(gate_pre, up_pre))
    return residual + jnp.dot(hidden, w_down, precision=highest) + b_down

def reference(x_in, cotangent, gain_mix, w_in, b_in, conv_w, conv_b, w_gates, b_gates, decay_param, w_out, b_out, gain_mlp, w_up, b_up, w_down, b_down):
    params = (gain_mix.astype(jnp.float32), w_in.astype(jnp.float32), b_in.astype(jnp.float32), conv_w.astype(jnp.float32), conv_b.astype(jnp.float32), w_gates.astype(jnp.float32), b_gates.astype(jnp.float32), decay_param.astype(jnp.float32), w_out.astype(jnp.float32), b_out.astype(jnp.float32), gain_mlp.astype(jnp.float32), w_up.astype(jnp.float32), b_up.astype(jnp.float32), w_down.astype(jnp.float32), b_down.astype(jnp.float32))

    def one_sequence(accumulated, item_pair):
        x_seq, cot_seq = item_pair
        result, pull_back = jax.vjp(forward, x_seq.astype(jnp.float32), *params)
        grads = pull_back(cot_seq.astype(jnp.float32))
        accumulated = jax.tree.map(jnp.add, accumulated, tuple(grads[1:]))
        return (accumulated, (result.astype(jnp.bfloat16), grads[0].astype(jnp.bfloat16)))
    seq_inputs = x_in.reshape(-1, x_in.shape[2], x_in.shape[3])
    seq_cots = cotangent.reshape(-1, x_in.shape[2], x_in.shape[3])
    zeros_start = tuple((jnp.zeros_like(param) for param in params))
    totals, (results, input_grads) = lax.scan(one_sequence, zeros_start, (seq_inputs, seq_cots))
    return (results.reshape(x_in.shape), input_grads.reshape(x_in.shape), totals[0], totals[1], totals[2], totals[3], totals[4], totals[5], totals[6], totals[7], totals[8], totals[9], totals[10], totals[11], totals[12], totals[13], totals[14])
```

```python
from functools import partial

import jax
import jax.numpy as jnp
from jax import lax
from jax.experimental import pallas as pl
from jax.experimental.pallas import tpu as pltpu
from jax.sharding import PartitionSpec as P

WIDTH = 2560
BW = 256
CONV = 4
LANES = 128
SEGMENTS = 8

EPSILON = 1e-06
DECAY_SCALE = 8.0
BF = jnp.bfloat16
F32 = jnp.float32


def moved(shard, axis, by):
    count = lax.axis_size(axis)
    pairs = [(i, i + by) for i in range(count) if 0 <= i + by < count]
    return lax.ppermute(shard, axis, pairs)


def turned(shard, axis, by):
    count = lax.axis_size(axis)
    return lax.ppermute(shard, axis, [(i, (i + by) % count) for i in range(count)])


def swapped(shard, axis, bit):
    count = lax.axis_size(axis)
    return lax.ppermute(shard, axis, [(i, i ^ bit) for i in range(count)])


def held_after(value, *others):
    return lax.optimization_barrier((value, *others))[0]


def block_of(rows, index, count):
    size = rows.shape[0] // count
    return lax.dynamic_slice_in_dim(rows, index * size, size, axis=0)


def gather_rows(own, other, place_dp, place_seq):
    count, dps = lax.axis_size("seq"), lax.axis_size("dp")
    rows, columns = own.shape
    whole = jnp.zeros((dps, count, rows, columns), own.dtype)
    for by in range(count):
        piece = own if by == 0 else turned(own if by % 2 == 0 else other, "seq", by)
        source = lax.rem(place_seq - by + count, count)
        partner = swapped(piece, "dp", 1)
        whole = lax.dynamic_update_slice(whole, piece[None, None], (place_dp, source, 0, 0))
        whole = lax.dynamic_update_slice(whole, partner[None, None], (1 - place_dp, source, 0, 0))
    return whole.reshape(dps * count * rows, columns)


def return_halves(to_partner, to_keep, place_seq):
    count = lax.axis_size("seq")
    rows = to_keep.shape[0] // count
    mine = (to_keep.astype(F32) + swapped(to_partner, "dp", 1).astype(F32)).astype(BF)
    halves = [block_of(mine, place_seq, count).astype(F32), None]
    for by in range(1, count):
        target = lax.rem(place_seq + by, count)
        came = turned(block_of(mine, target, count), "seq", by).astype(F32)
        halves[by % 2] = came if halves[by % 2] is None else halves[by % 2] + came
    return halves


def return_rows(to_partner, to_keep, place_seq):
    count = lax.axis_size("seq")
    mine = (to_keep.astype(F32) + swapped(to_partner, "dp", 1).astype(F32)).astype(BF)
    total = block_of(mine, place_seq, count).astype(F32)
    for by in range(1, count):
        target = lax.rem(place_seq + by, count)
        total = total + turned(block_of(mine, target, count), "seq", by).astype(F32)
    return total


def quarter_sums(blocks):
    total = blocks[0].astype(F32)
    for bit in range(1, len(blocks)):
        total = total + swapped(blocks[bit], "tensor", bit).astype(F32)
    return total


def quarter_copies(part):
    return [part] + [swapped(part, "tensor", bit) for bit in range(1, lax.axis_size("tensor"))]


def scan_kernel(reverse, decay_ref, drive_ref, state_ref, prod_ref, total_ref):
    count, length, channels = decay_ref.shape
    run = length // SEGMENTS

    def step(turn, carry):
        i = run - 1 - turn if reverse else turn
        rows = pl.ds(i, SEGMENTS, stride=run)
        after = []
        for b in range(count):
            state, prod = carry[b]
            decay = decay_ref[b, rows, :]
            drive = drive_ref[b, rows, :]
            if reverse:
                value = drive + state
                state_ref[b, rows, :] = value
                prod_ref[b, rows, :] = prod
                after.append((decay * value, prod * decay))
            else:
                state = decay * state + drive
                prod = prod * decay
                state_ref[b, rows, :] = state
                prod_ref[b, rows, :] = prod
                after.append((state, prod))
        return tuple(after)

    zero = jnp.zeros((SEGMENTS, channels), F32)
    ends = lax.fori_loop(0, run, step, ((zero, zero + 1.0),) * count, unroll=8)
    order = range(SEGMENTS - 1, -1, -1) if reverse else range(SEGMENTS)
    for b in range(count):
        state_end, prod_end = ends[b]
        state_in = jnp.zeros((1, channels), F32)
        prod_in = jnp.ones((1, channels), F32)
        for place, seg in enumerate(order):
            rows = pl.ds(seg * run, run)
            if place > 0:
                prod = prod_ref[b, rows, :]
                state_ref[b, rows, :] = state_ref[b, rows, :] + prod * state_in
                prod_ref[b, rows, :] = prod * prod_in
            state_in = prod_end[seg : seg + 1] * state_in + state_end[seg : seg + 1]
            prod_in = prod_end[seg : seg + 1] * prod_in
        total_ref[b, 0:1, :] = prod_in
        total_ref[b, 1:2, :] = state_in


def scan_runs(decays, drives, reverse):
    count, length, channels = decays.shape
    block = pl.BlockSpec((count, length, LANES), lambda c: (0, 0, c))
    return pl.pallas_call(
        partial(scan_kernel, reverse),
        grid=(channels // LANES,),
        in_specs=[block, block],
        out_specs=[block, block, pl.BlockSpec((count, 2, LANES), lambda c: (0, 0, c))],
        out_shape=[
            jax.ShapeDtypeStruct(decays.shape, F32),
            jax.ShapeDtypeStruct(decays.shape, F32),
            jax.ShapeDtypeStruct((count, 2, channels), F32),
        ],
        cost_estimate=pl.CostEstimate(
            flops=8 * decays.size, bytes_accessed=16 * decays.size, transcendentals=0
        ),
        name="scan_back" if reverse else "scan_fwd",
    )(decays, drives)


def entering(totals, reverse):
    count = lax.axis_size("seq")
    came = [moved(totals, "seq", -by if reverse else by) for by in range(1, count)]
    state = jnp.zeros_like(totals[:, 1])
    for one in reversed(came):
        state = one[:, 0] * state + one[:, 1]
    return state


def rms_scale(values, gain_vec):
    inverse = lax.rsqrt(jnp.mean(values * values, axis=-1, keepdims=True) + EPSILON)
    return values * inverse * gain_vec


def gelu_gate(gate_pre, up_pre):
    return jax.nn.gelu(gate_pre) * up_pre


def recurrence_terms(gate_rate, gate_input, inputs, decay_param, is_first):
    rate_gate = jax.nn.sigmoid(gate_rate)
    inward = jax.nn.sigmoid(gate_input)
    log_decay = -DECAY_SCALE * jax.nn.softplus(-decay_param) * rate_gate
    decays = jnp.exp(log_decay)
    factor = jnp.where(is_first, 1.0, jnp.sqrt(-jnp.expm1(2.0 * log_decay)))
    return (decays, factor * inward * inputs)


def dot_nn(a, b):
    return lax.dot_general(a, b, (((1,), (0,)), ((), ())), preferred_element_type=F32)


def dot_nt(a, b):
    return lax.dot_general(a, b, (((1,), (1,)), ((), ())), preferred_element_type=F32)


def dot_tn(a, b):
    return lax.dot_general(a, b, (((0,), (0,)), ((), ())), preferred_element_type=F32)


def row_sum(values):
    return jnp.sum(values.astype(F32), axis=0)


def gate_matrix(gates_all, in_block, row_onehot):
    rate_part = jnp.dot(row_onehot, gates_all[0], preferred_element_type=F32)
    input_part = jnp.dot(row_onehot, gates_all[1], preferred_element_type=F32)
    rate_part = jnp.where(in_block, rate_part, 0.0)
    input_part = jnp.where(in_block, input_part, 0.0)
    return jnp.concatenate([rate_part, input_part], axis=1).astype(BF)


def halves_of(values, width, is_low):
    low_part = values[..., :width]
    rest = values[..., width:]
    spare = [(0, 0)] * (values.ndim - 1) + [(0, 2 * width - values.shape[-1])]
    high_part = jnp.pad(rest, spare)
    return jnp.where(is_low, low_part, high_part), jnp.where(is_low, high_part, low_part)


def joined(own, other, is_low, columns):
    low_part = jnp.where(is_low, own, other)
    high_part = jnp.where(is_low, other, own)
    return jnp.concatenate([low_part, high_part[..., : columns - own.shape[-1]]], axis=-1)


def body(
    x_in,
    cotangent,
    gain_mix,
    w_in,
    b_in,
    conv_w,
    conv_b,
    w_gates,
    b_gates,
    decay_param,
    w_out,
    b_out,
    gain_mlp,
    w_up,
    b_up,
    w_down,
    b_down,
):
    micro_count, seqs_here, local_len, model_width = x_in.shape
    runs = micro_count * seqs_here
    tokens = runs * local_len
    width_dev = w_in.shape[2]
    rows_dev = w_in.shape[1]
    hidden_dev = w_up.shape[2]
    dps, seqs, tensors = lax.axis_size("dp"), lax.axis_size("seq"), lax.axis_size("tensor")
    place_dp, place_seq = lax.axis_index("dp"), lax.axis_index("seq")
    place_t = lax.axis_index("tensor")
    is_low = lax.rem(place_seq, 2) == 0
    part = -(-hidden_dev // (2 * LANES)) * LANES
    dp_rows = model_width // dps
    quarter = tokens // tensors

    rim_chan = min(BW, width_dev)
    ext_rows = width_dev + 2 * rim_chan
    column_start = place_t * width_dev
    row_global = column_start - rim_chan + lax.broadcasted_iota(jnp.int32, (ext_rows, width_dev), 0)
    col_global = column_start + lax.broadcasted_iota(jnp.int32, (ext_rows, width_dev), 1)
    in_block = (
        (row_global >= 0)
        & (row_global < WIDTH)
        & (jnp.floor_divide(row_global, BW) == col_global // BW)
    )
    row_in_block = jnp.mod(row_global[:, 0], BW)
    block_pos = lax.broadcasted_iota(jnp.int32, (ext_rows, BW), 1)
    onehot_f = (row_in_block[:, None] == block_pos).astype(F32)
    row_onehot = onehot_f.astype(BF)
    time_pos = lax.broadcasted_iota(jnp.int32, (1, local_len, 1), 1)
    is_first = (time_pos == 0) & (place_seq == 0)
    lru_terms = partial(recurrence_terms, is_first=is_first)
    rim_width = CONV - 1
    gate_bias = b_gates.reshape(-1)

    w_in_all = lax.all_gather(w_in, ("dp", "seq"), axis=1, tiled=True)
    w_out_t = lax.all_gather(w_out.T, ("dp", "seq"), axis=0, tiled=True)
    gate_rows = w_gates.shape[1]
    gates_flat = w_gates.reshape(2 * gate_rows, width_dev)
    gates_all = gather_rows(gates_flat, gates_flat, place_dp, place_seq)
    gates_all = gates_all.reshape(dps * seqs, 2, gate_rows, width_dev)
    gates_all = jnp.swapaxes(gates_all, 0, 1).reshape(2, BW, width_dev)

    up_own, up_other = halves_of(w_up, part, is_low)
    up_own = jnp.concatenate([up_own[0], up_own[1]], axis=1)
    up_other = jnp.concatenate([up_other[0], up_other[1]], axis=1)
    down_own, down_other = halves_of(w_down.T, part, is_low)
    up_own, up_other, down_own, down_other, w_in_all = lax.optimization_barrier(
        (up_own, up_other, down_own, down_other, w_in_all)
    )
    w_up_all = gather_rows(up_own, up_other, place_dp, place_seq)
    w_down_all = gather_rows(down_own, down_other, place_dp, place_seq)
    up_bias = halves_of(b_up, part, is_low)[0]

    cot_rows = cotangent.reshape(tokens, model_width)
    cot_quarter = block_of(cot_rows, place_t, tensors)
    cot_own = [block_of(cot_rows, place_t ^ bit, tensors) for bit in range(tensors)]
    cot_pair = quarter_copies(swapped(cot_quarter, "seq", 1))
    cot_all = jnp.concatenate(cot_own + cot_pair, axis=0)

    x_rows = x_in.reshape(tokens, model_width)
    normed = rms_scale(x_rows.astype(F32), gain_mix).astype(BF)
    x_low = (dot_nn(normed, w_in_all[1]) + b_in[1]).astype(BF).reshape(runs, local_len, width_dev)
    y_pre = (dot_nn(normed, w_in_all[0]) + b_in[0]).reshape(runs, local_len, width_dev)
    before = moved(x_low[:, local_len - rim_width :, :], "seq", 1)
    extended = jnp.concatenate([before, x_low], axis=1).astype(F32)
    conv_out = conv_b + conv_w[0] * extended[:, 0:local_len]
    for offset in range(1, CONV):
        conv_out = conv_out + conv_w[offset] * extended[:, offset : offset + local_len]
    conv_low = conv_out.astype(BF)
    conv_vals = conv_low.astype(F32)
    from_left = moved(conv_low[:, :, width_dev - rim_chan :], "tensor", 1)
    from_right = moved(conv_low[:, :, :rim_chan], "tensor", -1)
    window = jnp.concatenate([from_left, conv_low, from_right], axis=2).reshape(tokens, ext_rows)
    matrix = gate_matrix(gates_all, in_block, row_onehot)
    gate_values = (dot_nn(window, matrix) + gate_bias).reshape(runs, local_len, 2 * width_dev)
    gate_rate = gate_values[..., :width_dev]
    gate_input = gate_values[..., width_dev:]
    decays, drives = lru_terms(gate_rate, gate_input, conv_vals, decay_param)
    local_state, cum_decay, run_total = scan_runs(decays, drives, False)
    state_in = entering(run_total, False)
    states = local_state + cum_decay * state_in[:, None]
    branch = jax.nn.gelu(y_pre)
    mixed_out = (states * branch).astype(BF).reshape(tokens, width_dev)
    mix_part = dot_nt(mixed_out, w_out_t).astype(BF)
    mix_sum = quarter_sums([block_of(mix_part, place_t ^ bit, tensors) for bit in range(tensors)])
    x_quarter = block_of(x_rows, place_t, tensors).astype(F32)
    residual = x_quarter + (mix_sum + b_out)

    normed_two_q = rms_scale(residual, gain_mlp).astype(BF)
    normed_two = jnp.concatenate(
        quarter_copies(normed_two_q) + quarter_copies(swapped(normed_two_q, "seq", 1)), axis=0
    )
    pre = dot_nn(normed_two, w_up_all)
    gate_pre = pre[:, :part] + up_bias[0]
    up_pre = pre[:, part:] + up_bias[1]
    hidden = gelu_gate(gate_pre, up_pre).astype(BF)

    def pair_sum(values):
        blocks = [block for block in jnp.split(values.astype(BF), 2 * tensors, axis=0)]
        for_pair = quarter_sums(blocks[tensors:]).astype(BF)
        return quarter_sums(blocks[:tensors]) + swapped(for_pair, "seq", 1).astype(F32)

    def two_parts(left_side, right_side):
        to_partner = lax.dynamic_slice_in_dim(left_side, (1 - place_dp) * dp_rows, dp_rows, axis=1)
        to_keep = lax.dynamic_slice_in_dim(left_side, place_dp * dp_rows, dp_rows, axis=1)
        return dot_tn(to_partner, right_side).astype(BF), dot_tn(to_keep, right_side).astype(BF)

    down_halves = return_halves(*two_parts(cot_all, hidden), place_seq)
    grad_hidden = dot_nn(cot_all, w_down_all)
    grad_gate, grad_up = jax.vjp(gelu_gate, gate_pre, up_pre)[1](grad_hidden)
    grad_pre = jnp.concatenate([grad_gate.astype(BF), grad_up.astype(BF)], axis=1)
    grad_normed_two = pair_sum(dot_nt(grad_pre, w_up_all))
    up_halves = return_halves(*two_parts(normed_two, grad_pre), place_seq)
    grad_b_up = row_sum(grad_pre).reshape(2, part)
    down_sum = pair_sum(dot_nt(hidden, w_down_all))
    out_quarter = (residual + down_sum + b_down).astype(BF)
    block_out = lax.all_gather(out_quarter, "tensor", axis=0, tiled=True).reshape(x_in.shape)

    grad_resid_norm, grad_gain_mlp = jax.vjp(rms_scale, residual, gain_mlp)[1](grad_normed_two)
    grad_residual = cot_quarter.astype(F32) + grad_resid_norm
    grad_mix_q = grad_residual.astype(BF)
    grad_b_down = row_sum(cot_quarter)
    grad_b_out = row_sum(grad_mix_q)
    grad_mix = jnp.zeros((tokens, model_width), BF)
    for bit, copy in enumerate(quarter_copies(grad_mix_q)):
        grad_mix = lax.dynamic_update_slice_in_dim(grad_mix, copy, (place_t ^ bit) * quarter, 0)

    grad_mixed = dot_nn(grad_mix, w_out_t).reshape(runs, local_len, width_dev)
    out_rows = return_rows(*two_parts(grad_mix, mixed_out), place_seq)
    grad_states = grad_mixed * branch
    grad_y = jax.vjp(jax.nn.gelu, y_pre)[1](grad_mixed * states)[0].astype(BF)
    local_adj, cum_next, back_total = scan_runs(decays, grad_states, True)
    adjoint = local_adj + cum_next * entering(back_total, True)[:, None]
    prev_state = jnp.concatenate([state_in[:, None], states[:, :-1]], axis=1)
    grad_rate, grad_inward, grad_conv, grad_decay = jax.vjp(
        lru_terms, gate_rate, gate_input, conv_vals, decay_param
    )[1]((adjoint * prev_state, adjoint))
    grad_gates = jnp.concatenate([grad_rate, grad_inward], axis=-1).astype(BF)
    grad_gates = grad_gates.reshape(tokens, 2 * width_dev)
    grad_window = dot_nt(grad_gates, matrix).reshape(runs, local_len, ext_rows)
    from_right = moved(grad_window[..., :rim_chan].astype(BF), "tensor", -1).astype(F32)
    from_left = moved(grad_window[..., rim_chan + width_dev :].astype(BF), "tensor", 1).astype(F32)
    own_part = grad_window[..., rim_chan : rim_chan + width_dev]
    spare = width_dev - rim_chan
    grad_conv = (
        grad_conv
        + own_part
        + jnp.pad(from_left, ((0, 0), (0, 0), (0, spare)))
        + jnp.pad(from_right, ((0, 0), (0, 0), (spare, 0)))
    )
    grad_conv_b = jnp.sum(grad_conv, axis=(0, 1))
    grad_conv_w = jnp.stack(
        [
            jnp.sum(grad_conv * extended[:, offset : offset + local_len], axis=(0, 1))
            for offset in range(CONV)
        ]
    )
    from_next = moved(grad_conv[:, :rim_width], "seq", -1)
    grad_ext = jnp.concatenate([grad_conv, from_next], axis=1)
    grad_x_pre = conv_w[CONV - 1] * grad_conv
    for offset in range(1, CONV):
        grad_x_pre = grad_x_pre + conv_w[CONV - 1 - offset] * grad_ext[:, offset : offset + local_len]
    grad_x_low = grad_x_pre.astype(BF).reshape(tokens, width_dev)
    grad_y = grad_y.reshape(tokens, width_dev)
    grad_in = jnp.concatenate([grad_y, grad_x_low], axis=1)
    grad_b_in = row_sum(grad_in).reshape(2, width_dev)
    in_rows = return_rows(*two_parts(normed, grad_in), place_seq)
    normed_part = dot_nt(grad_y, w_in_all[0]) + dot_nt(grad_x_low, w_in_all[1])
    normed_part = normed_part.astype(BF)
    grad_normed = quarter_sums(
        [block_of(normed_part, place_t ^ bit, tensors) for bit in range(tensors)]
    )
    grad_inputs_norm, grad_gain_mix = jax.vjp(rms_scale, x_quarter, gain_mix)[1](grad_normed)
    input_quarter = (grad_residual + grad_inputs_norm).astype(BF)
    grad_input = lax.all_gather(input_quarter, "tensor", axis=0, tiled=True).reshape(x_in.shape)

    grad_matrix = dot_tn(window, grad_gates)
    folded = jnp.stack([grad_matrix[:, :width_dev], grad_matrix[:, width_dev:]])
    folded = jnp.where(in_block[None], folded, 0.0)
    grad_w_gates = jnp.einsum("kj,gkc->gjc", onehot_f, folded, precision=lax.Precision.HIGHEST)
    gate_parts = grad_w_gates.astype(BF).reshape(2, dps, seqs * gate_rows, width_dev)
    gate_parts = jnp.moveaxis(gate_parts, 0, 1).reshape(dps, 2, seqs, gate_rows, width_dev)
    gate_parts = jnp.swapaxes(gate_parts, 1, 2).reshape(dps, seqs * 2 * gate_rows, width_dev)
    gates_total = return_rows(
        lax.dynamic_index_in_dim(gate_parts, 1 - place_dp, 0, False),
        lax.dynamic_index_in_dim(gate_parts, place_dp, 0, False),
        place_seq,
    ).reshape(2, gate_rows, width_dev)

    bias_low = jnp.where(is_low, grad_b_up, 0.0)
    bias_high = jnp.where(is_low, 0.0, grad_b_up)
    over_rows = [grad_b_in, grad_conv_w, grad_conv_b, grad_b_gates_of(grad_gates), grad_decay,
                 bias_low, bias_high]
    over_all = [grad_gain_mix, grad_b_out, grad_gain_mlp, grad_b_down]

    def packed(values):
        flat = jnp.concatenate([value.reshape(-1) for value in values])
        return flat.reshape(-1, LANES)

    rows_pack, all_pack = packed(over_rows), packed(over_all)
    split = rows_pack.shape[0]
    bit = 1
    while bit < tensors:
        all_pack = all_pack + swapped(all_pack, "tensor", bit)
        bit *= 2
    pack = jnp.concatenate([rows_pack, all_pack], axis=0)
    for axis, count in (("dp", dps), ("seq", seqs)):
        bit = 1
        while bit < count:
            pack = pack + swapped(pack, axis, bit)
            bit *= 2

    def unpacked(flat, values):
        outs, start = [], 0
        for value in values:
            outs.append(flat[start : start + value.size].reshape(value.shape))
            start += value.size
        return outs

    sum_b_in, sum_conv_w, sum_conv_b, sum_b_gates, sum_decay, sum_low, sum_high = unpacked(
        pack[:split].reshape(-1), over_rows
    )
    sum_gain_mix, sum_b_out, sum_gain_mlp, sum_b_down = unpacked(
        pack[split:].reshape(-1), over_all
    )
    sum_b_up = jnp.concatenate([sum_low, sum_high[:, : hidden_dev - part]], axis=1)

    grad_up_rows = [
        joined(up_halves[0][:, g * part : (g + 1) * part], up_halves[1][:, g * part : (g + 1) * part],
               is_low, hidden_dev)
        for g in range(2)
    ]
    grad_down_rows = joined(down_halves[0], down_halves[1], is_low, hidden_dev)
    grad_in_rows = jnp.stack([in_rows[:, :width_dev], in_rows[:, width_dev:]])
    return (
        block_out,
        grad_input,
        sum_gain_mix,
        grad_in_rows,
        sum_b_in,
        sum_conv_w,
        sum_conv_b,
        gates_total,
        sum_b_gates.reshape(2, width_dev),
        sum_decay,
        out_rows.T,
        sum_b_out,
        sum_gain_mlp,
        jnp.stack(grad_up_rows),
        sum_b_up,
        grad_down_rows.T,
        sum_b_down,
    )


def grad_b_gates_of(grad_gates):
    return row_sum(grad_gates)


def solution(mesh):
    rows_and_tensor = P(None, ("dp", "seq"), "tensor")
    placed = (
        P(None, "dp", "seq", None),
        P(None, "dp", "seq", None),
        P(),
        rows_and_tensor,
        P(None, "tensor"),
        P(None, "tensor"),
        P("tensor"),
        rows_and_tensor,
        P(None, "tensor"),
        P("tensor"),
        P("tensor", ("dp", "seq")),
        P(),
        P(),
        rows_and_tensor,
        P(None, "tensor"),
        P("tensor", ("dp", "seq")),
        P(),
    )
    return jax.shard_map(
        body,
        mesh=mesh,
        in_specs=placed,
        out_specs=(
            P(None, "dp", "seq", None),
            P(None, "dp", "seq", None),
            P(),
            rows_and_tensor,
            P(None, "tensor"),
            P(None, "tensor"),
            P("tensor"),
            rows_and_tensor,
            P(None, "tensor"),
            P("tensor"),
            P("tensor", ("dp", "seq")),
            P(),
            P(),
            rows_and_tensor,
            P(None, "tensor"),
            P("tensor", ("dp", "seq")),
            P(),
        ),
        check_vma=False,
    )
```
